32 devices in a mesh: row: 4 (over y, core), col: 8 (over z, x).
Axes of the slice: x: 2, y: 2, z: 4, core: 2. Of those that a mesh axis runs over, the one named last changes fastest.
Arguments:
- left: bfloat16 [128, 8192], P('col', 'row'), may hold values from -6 to 6
- right: bfloat16 [128, 8192], P('row', 'col'), may hold values from -6 to 6
- proj: bfloat16 [1024, 128], replicated, may hold values from -2 to 2
- bias: float32 [128], replicated, may hold values from -1 to 1
- pair_grad: bfloat16 [256, 256, 128], P('row', 'col'), may hold values from -0.1875 to 0.1875
Outputs:
- pair_out: bfloat16 [256, 256, 128], P('row', 'col')
- left_grad: float32 [128, 8192], P('col', 'row')
- right_grad: float32 [128, 8192], P('row', 'col')
- proj_grad: float32 [1024, 128], replicated
The draws below stay inside these ranges and needn't reach their ends.
All inputs are finite; a program needn't handle non-finite values.
Results may differ from the reference program's by a relative error of at most 0.0056.
Values may be sent and summed in bfloat16 or wider, within the bound.
A program may use at most 128 MiB of HBM per device.

```python
import jax
import jax.numpy as jnp
from jax import lax

CH = 32
PAIR = 128
SEQS = 128
TOK_DEV = 64
OUTER = 1024
TOKENS = 256


def shard_levels(rng, dims, cuts, smallest, high):
    factor_of = 1.0
    for axis_at, parts in cuts:
        steps = jax.random.uniform(jax.random.fold_in(jax.random.fold_in(rng, 6), axis_at), (parts,), jnp.float32, smallest / len(cuts), high / len(cuts))
        factor_of = factor_of * jnp.repeat(jnp.exp(steps), dims[axis_at] // parts).reshape((-1,) + (1,) * (len(dims) - 1 - axis_at))
    return factor_of


def gaussian(stream_key, dims, deviation, limit, cuts=(), held_as=jnp.bfloat16):
    array = deviation * jax.random.normal(stream_key, dims, jnp.float32)
    if cuts:
        array = array * shard_levels(stream_key, dims, cuts, -0.22, 0.18)
    return jnp.clip(array, -limit, limit).astype(held_as)


def setup_inputs(seed: int = 0) -> dict:
    key_of = jax.random.split(jax.random.key(seed), 6)
    left = gaussian(key_of[0], (SEQS, TOKENS * CH), 1.0, 6.0, ((0, 8), (1, 4)))
    right = gaussian(key_of[1], (SEQS, TOKENS * CH), 1.0, 6.0, ((0, 4), (1, 8)))
    proj = gaussian(key_of[2], (OUTER, PAIR), (OUTER // SEQS) ** -0.5, 2.0)
    bias = jnp.clip(jax.random.uniform(key_of[3], (PAIR,), jnp.float32, -1.0, 1.0), -1.0, 1.0)
    pair_grad = gaussian(key_of[4], (TOKENS, TOKENS, PAIR), 0.03, 0.1875, ((0, 4), (1, 8)))
    return {"left": left, "right": right, "proj": proj, "bias": bias, "pair_grad": pair_grad}


def reference(left, right, proj, bias, pair_grad):
    left_cube = left.reshape(SEQS, TOKENS, CH)
    right_cube = right.reshape(SEQS, TOKENS, CH)
    right_wide = right_cube.astype(jnp.float32)
    blocks = TOKENS // TOK_DEV

    def step_block(totals, index_block):
        weight_total, right_total = totals
        first_row = (index_block * TOK_DEV).astype(jnp.int32)
        left_block = lax.dynamic_slice_in_dim(left_cube, first_row, TOK_DEV, 1)
        grad_block = lax.dynamic_slice_in_dim(pair_grad, first_row, TOK_DEV, 0)
        outers = jnp.einsum('sic,sje->ijce', left_block.astype(jnp.float32), right_wide) / SEQS
        outers = outers.astype(jnp.bfloat16).reshape(TOK_DEV * TOKENS, OUTER)
        preact = jnp.dot(outers, proj, preferred_element_type=jnp.float32) + bias
        active = jnp.maximum(preact, 0.0)
        pair_block = (active * active).astype(jnp.bfloat16).reshape(TOK_DEV, TOKENS, PAIR)
        grad_pre = (grad_block.reshape(TOK_DEV * TOKENS, PAIR).astype(jnp.float32) * 2.0 * active).astype(jnp.bfloat16)
        weight_total = weight_total + jnp.dot(outers.T, grad_pre, preferred_element_type=jnp.float32)
        grad_outer = jnp.dot(grad_pre, proj.T, preferred_element_type=jnp.float32).astype(jnp.bfloat16)
        grad_outer = grad_outer.reshape(TOK_DEV, TOKENS, CH, CH).astype(jnp.float32)
        left_block_grad = jnp.einsum('ijce,sje->sic', grad_outer, right_wide) / SEQS
        right_total = right_total + jnp.einsum('ijce,sic->sje', grad_outer, left_block.astype(jnp.float32)) / SEQS
        return (weight_total, right_total), (pair_block, left_block_grad)

    start = (jnp.zeros((OUTER, PAIR), jnp.float32), jnp.zeros((SEQS, TOKENS, CH), jnp.float32))
    (proj_grad, right_total), (pair_blocks, left_blocks) = lax.scan(step_block, start, jnp.arange(blocks, dtype=jnp.int32))
    pair_out = pair_blocks.reshape(TOKENS, TOKENS, PAIR)
    left_grad = jnp.transpose(left_blocks, (1, 0, 2, 3)).reshape(SEQS, TOKENS * CH)
    right_grad = right_total.reshape(SEQS, TOKENS * CH)
    return pair_out, left_grad, right_grad, proj_grad
```

```python
import functools

import jax
import jax.numpy as jnp
from jax import lax
from jax.experimental import pallas as pl
from jax.experimental.pallas import tpu as pltpu
from jax.sharding import PartitionSpec as P

CH = 32
PAIR = 128
LANES = 128
PACK = LANES // CH
WIDE = PACK * LANES
TILE = 256
MESH = pl.DeviceIdType.MESH
F32 = jnp.float32
BF16 = jnp.bfloat16


def inner_size(n):
    inner = 1
    while inner * inner * 4 <= n and n % (inner * 2) == 0:
        inner *= 2
    return inner


def dot(a, b):
    return jnp.dot(a, b, preferred_element_type=F32)


def aligned(index, size):
    return pl.ds(pl.multiple_of(index * size, size), size)


def kernel(
    R, C, share,
    left, right, proj, bias, pair_grad,
    pair_out, left_out, right_out, proj_out,
    lbuf, rbuf, lfull, ltrans, rtrans, rperm_t, rperm,
    pfull, spread, spread_t, outer, gpre, gpre_t, gouter,
    pterm, psend, precv, psum, pshare, pparts, pgather,
    rtmp, rown, rsend, rparts, lown, lsend, lxparts, lzsend, lzparts,
    s_lz, r_lz, s_lx, r_lx, s_rg, r_rg,
    s_pc, r_pc, s_ps, r_ps, s_pa, r_pa, s_pe, r_pe,
    s_rs, r_rs, s_lsx, r_lsx, s_lsz, r_lsz,
):
    C2 = inner_size(C)
    C1 = C // C2
    row, col = lax.axis_index("row"), lax.axis_index("col")
    z, x = col // C2, lax.rem(col, C2)
    seqs = lfull.shape[0]
    lwide = left.shape[1]
    rwide = right.shape[1]
    cols_here = rwide // CH
    groups = lwide // LANES
    rows = groups * cols_here
    scale = 1.0 / seqs

    def send(src, dst, ssem, rsem, to_row, to_col):
        return pltpu.make_async_remote_copy(
            src_ref=src, dst_ref=dst, send_sem=ssem, recv_sem=rsem,
            device_id=(to_row, to_col), device_id_type=MESH,
        )

    def zpeer(d):
        return lax.rem(z + d, C1)

    def xpeer(d):
        return lax.rem(x + d, C2)

    def rpeer(d):
        return lax.rem(row + d, R)

    barrier = pltpu.get_barrier_semaphore()
    for d in range(1, R):
        pl.semaphore_signal(barrier, inc=1, device_id=(rpeer(d), col), device_id_type=MESH)
    for d in range(1, C2):
        pl.semaphore_signal(
            barrier, inc=1, device_id=(row, z * C2 + xpeer(d)), device_id_type=MESH)
    for d in range(1, C1):
        pl.semaphore_signal(
            barrier, inc=1, device_id=(row, zpeer(d) * C2 + x), device_id_type=MESH)
    pl.semaphore_wait(barrier, R - 1 + C1 - 1 + C2 - 1)

    pending = []

    def go(copy):
        copy.start()
        pending.append(copy)
        return copy

    for d in range(1, R):
        go(send(right, rbuf.at[row], s_rg.at[d - 1], r_rg.at[d - 1], rpeer(d), col))
    for d in range(1, C1):
        go(send(left, lbuf.at[col], s_lz.at[d - 1], r_lz.at[d - 1], row, zpeer(d) * C2 + x))
    for d in range(1, C2):
        go(send(left, lbuf.at[col], s_lx.at[d - 1, 0], r_lx.at[d - 1, 0], row, z * C2 + xpeer(d)))

    lbuf[col] = left[...]
    rbuf[row] = right[...]
    pfull[...] = proj[...].astype(F32)
    lane_of = lax.broadcasted_iota(jnp.int32, (LANES, LANES), 1) // CH
    zero = jnp.zeros((CH, LANES), BF16)

    @pl.loop(0, CH)
    def _(e):
        block = pfull[pl.ds(e, CH, stride=CH), :]
        narrow = block.astype(BF16)
        spread[aligned(e, LANES), :] = jnp.concatenate(
            [
                jnp.concatenate([narrow if a == b else zero for b in range(PACK)], axis=1)
                for a in range(PACK)
            ],
            axis=0,
        )
        turned = jnp.concatenate([block] * PACK, axis=0).T
        for a in range(PACK):
            spread_t[a * LANES:(a + 1) * LANES, aligned(e, LANES)] = jnp.where(
                lane_of == a, turned, 0.0
            ).astype(BF16)

    for d in range(1, C1):
        block = lax.rem(z + C1 - d, C1) * C2 + x
        send(left, lbuf.at[block], s_lz.at[d - 1], r_lz.at[d - 1], row, col).wait_recv()
        for k in range(1, C2):
            go(send(
                lbuf.at[block], lbuf.at[block], s_lx.at[k - 1, d], r_lx.at[k - 1, d],
                row, z * C2 + xpeer(k)))
    for d in range(1, R):
        source = lax.rem(row + R - d, R)
        send(right, rbuf.at[source], s_rg.at[d - 1], r_rg.at[d - 1], row, col).wait_recv()

    rtrans[...] = rbuf[...].astype(F32).reshape(seqs, rwide).T

    @pl.loop(0, CH)
    def _(e):
        rperm_t[aligned(e, cols_here), :] = rtrans[
            pl.ds(e, cols_here, stride=CH), :].astype(BF16)

    rperm[...] = rperm_t[...].astype(F32).T.astype(BF16)

    for d in range(C1):
        for k in range(1, C2):
            block = lax.rem(z + C1 - d, C1) * C2 + lax.rem(x + C2 - k, C2)
            send(left, lbuf.at[block], s_lx.at[k - 1, d], r_lx.at[k - 1, d], row, col).wait_recv()
    whole_left = lbuf[...].astype(F32).reshape(seqs, lwide)
    lfull[...] = whole_left.astype(BF16)

    @pl.loop(0, lwide // TILE)
    def _(t):
        part = (dot(rperm_t[...], lfull[:, aligned(t, TILE)]) * scale).astype(BF16)
        for h in range(TILE // LANES):
            for e in range(CH):
                outer[aligned(t * (TILE // LANES) + h, cols_here), e * LANES:(e + 1) * LANES] = (
                    part[e * cols_here:(e + 1) * cols_here, h * LANES:(h + 1) * LANES])

    wide_bias = jnp.concatenate([bias[...]] * PACK, axis=1)

    @pl.loop(0, rows // TILE)
    def _(t):
        preact = dot(outer[aligned(t, TILE), :], spread[...]) + wide_bias
        active = jnp.maximum(preact, 0.0)
        square = (active * active).astype(BF16)
        per = TILE // cols_here
        for g in range(per):
            for a in range(PACK):
                token = (t * per + g) * PACK + a
                here = slice(g * cols_here, (g + 1) * cols_here)
                there = slice(a * LANES, (a + 1) * LANES)
                pair_out[token] = square[here, there]
                gpre[aligned(t * per + g, cols_here), there] = (
                    pair_grad[token].astype(F32) * 2.0 * active[here, there]).astype(BF16)
        gpre_t[:, aligned(t, TILE)] = gpre[aligned(t, TILE), :].astype(F32).T.astype(BF16)

    @pl.loop(0, CH * LANES // TILE)
    def _(t):
        part = dot(gpre_t[...], outer[:, aligned(t, TILE)])
        for h in range(TILE // LANES):
            lanes = slice(h * LANES, (h + 1) * LANES)
            picked = part[:LANES, lanes]
            for a in range(1, PACK):
                picked = jnp.where(lane_of == a, part[a * LANES:(a + 1) * LANES, lanes], picked)
            turned = picked.T
            total = turned[:CH]
            for a in range(1, PACK):
                total = total + turned[a * CH:(a + 1) * CH]
            pterm[aligned(t * (TILE // LANES) + h, CH), :] = total

    if share:
        half = pterm.shape[0] // 2
        core = lax.rem(row, 2)
        other = row + 1 - 2 * core
        count = half // share
        me = (row // 2) * C + col
        mine = pterm[aligned(core, half), :]
        psend[...] = pterm[aligned(1 - core, half), :].astype(BF16)
        swap = go(send(psend, precv, s_pc, r_pc, other, col))

    @pl.loop(0, CH * LANES // TILE)
    def _(t):
        part = dot(gpre[...], spread_t[:, aligned(t, TILE)]).astype(BF16)
        for h in range(TILE // LANES):
            for g in range(groups):
                gouter[aligned(t * (TILE // LANES) + h, cols_here), g * LANES:(g + 1) * LANES] = (
                    part[g * cols_here:(g + 1) * cols_here, h * LANES:(h + 1) * LANES])

    if share:
        def owner(k):
            return (k // C) * 2 + core, lax.rem(k, C)

        swap.wait_recv()
        both = (pterm[aligned(core, half), :] + precv[...].astype(F32)).reshape(count, share, PAIR)
        psum[...] = both
        pshare[...] = both.astype(BF16)
        scatter = []
        for d in range(1, count):
            k = lax.rem(me + d, count)
            scatter.append(go(send(
                pshare.at[k], pparts.at[d - 1], s_ps.at[d - 1], r_ps.at[d - 1], *owner(k))))

    @pl.loop(0, lwide // TILE)
    def _(t):
        part = (dot(rperm[...], gouter[:, aligned(t, TILE)]) * scale).reshape(
            C, seqs // C, TILE)
        lown[:, :, aligned(t, TILE)] = part
        lsend[:, :, aligned(t, TILE)] = part.astype(BF16)

    inner = []
    for k in range(1, C2):
        for d in list(range(1, C1)) + [0]:
            inner.append(go(send(
                lsend.at[zpeer(d) * C2 + xpeer(k)], lxparts.at[k - 1, d],
                s_lsx.at[k - 1, d], r_lsx.at[k - 1, d], row, z * C2 + xpeer(k))))

    ltrans[...] = lfull[...].astype(F32).T.astype(BF16)

    @pl.loop(0, CH * cols_here // TILE)
    def _(t):
        part = dot(gouter[aligned(t, TILE), :], ltrans[...]) * scale
        per = TILE // cols_here
        for k in range(per):
            rtmp[pl.ds(t * per + k, cols_here, stride=CH), :] = (
                part[k * cols_here:(k + 1) * cols_here])

    turned = rtmp[...].T.reshape(R, seqs // R, rwide)
    rown[...] = turned
    rsend[...] = turned.astype(BF16)
    rights = [
        go(send(rsend.at[rpeer(d)], rparts.at[d - 1], s_rs.at[d - 1], r_rs.at[d - 1], rpeer(d), col))
        for d in range(1, R)
    ]

    if share:
        for copy in scatter:
            copy.wait_recv()
        total = psum[me]
        for d in range(1, count):
            total = total + pparts[d - 1].astype(F32)
        pgather[core, me] = total.astype(BF16)
        for d in range(1, count):
            k = lax.rem(me + d, count)
            go(send(
                pgather.at[core, me], pgather.at[core, me], s_pa.at[d - 1], r_pa.at[d - 1],
                *owner(k)))
    else:
        proj_out[...] = pterm[...]

    for copy in inner:
        copy.wait_recv()
    outers = []
    for d in range(1, C1):
        total = lown[zpeer(d) * C2 + x]
        for k in range(1, C2):
            total = total + lxparts[k - 1, d].astype(F32)
        lzsend[d - 1] = total.astype(BF16)
        outers.append(go(send(
            lzsend.at[d - 1], lzparts.at[d - 1], s_lsz.at[d - 1], r_lsz.at[d - 1],
            row, zpeer(d) * C2 + x)))

    for copy in rights:
        copy.wait_recv()
    total = rown[row]
    for d in range(1, R):
        total = total + rparts[d - 1].astype(F32)
    right_out[...] = total

    if share:
        for d in range(1, count):
            k = lax.rem(me + count - d, count)
            send(
                pgather.at[core, me], pgather.at[core, k], s_pa.at[d - 1], r_pa.at[d - 1],
                *owner(k)).wait_recv()
        swap = go(send(pgather.at[core], pgather.at[core], s_pe, r_pe, other, col))

    total = lown[col]
    for k in range(1, C2):
        total = total + lxparts[k - 1, 0].astype(F32)
    for d, copy in enumerate(outers):
        copy.wait_recv()
        total = total + lzparts[d].astype(F32)
    left_out[...] = total

    if share:
        send(pgather.at[core], pgather.at[1 - core], s_pe, r_pe, other, col).wait_recv()
        rtmp_rows = pgather[...].astype(F32).reshape(2 * half, PAIR)
        pfull[...] = rtmp_rows

        @pl.loop(0, CH)
        def _(e):
            proj_out[pl.ds(e, CH, stride=CH), :] = pfull[aligned(e, CH), :]

    for copy in pending:
        copy.wait_send()


def solution(mesh):
    R, C = mesh.shape["row"], mesh.shape["col"]

    def step(left, right, proj, bias, pair_grad):
        lseq, lwide = left.shape
        rseq, rwide = right.shape
        seqs = lseq * C
        outer_size = proj.shape[0]
        cols_here = rwide // CH
        rows = lwide // LANES * cols_here
        C2 = inner_size(C)
        C1 = C // C2
        share = outer_size // (R * C) if R % 2 == 0 else 0
        if share % 16:
            share = 0
        half = outer_size // 2
        keep = share or half
        count = half // keep
        some = max(count - 1, 1)
        dma = pltpu.SemaphoreType.DMA
        V = pltpu.VMEM
        scratch = [
            V((C, lseq, lwide), BF16), V((R, rseq, rwide), BF16), V((seqs, lwide), BF16),
            V((lwide, seqs), BF16), V((rwide, seqs), F32), V((rwide, seqs), BF16),
            V((seqs, rwide), BF16),
            V((outer_size, PAIR), F32), V((PACK * outer_size, WIDE), BF16),
            V((WIDE, PACK * outer_size), BF16), V((rows, PACK * outer_size), BF16),
            V((rows, WIDE), BF16), V((WIDE, rows), BF16), V((rwide, lwide), BF16),
            V((outer_size, PAIR), F32), V((half, PAIR), BF16), V((half, PAIR), BF16),
            V((count, keep, PAIR), F32), V((count, keep, PAIR), BF16),
            V((some, keep, PAIR), BF16), V((2, count, keep, PAIR), BF16),
            V((rwide, seqs), F32), V((R, rseq, rwide), F32), V((R, rseq, rwide), BF16),
            V((R - 1, rseq, rwide), BF16),
            V((C, lseq, lwide), F32), V((C, lseq, lwide), BF16),
            V((C2 - 1, C1, lseq, lwide), BF16), V((C1 - 1, lseq, lwide), BF16),
            V((C1 - 1, lseq, lwide), BF16),
            dma((C1 - 1,)), dma((C1 - 1,)), dma((C2 - 1, C1)), dma((C2 - 1, C1)),
            dma((R - 1,)), dma((R - 1,)),
            dma, dma, dma((some,)), dma((some,)), dma((some,)), dma((some,)), dma, dma,
            dma((R - 1,)), dma((R - 1,)), dma((C2 - 1, C1)), dma((C2 - 1, C1)),
            dma((C1 - 1,)), dma((C1 - 1,)),
        ]
        vmem = pl.BlockSpec(memory_space=pltpu.VMEM)
        pair_out, left_grad, right_grad, proj_grad = pl.pallas_call(
            functools.partial(kernel, R, C, share),
            out_shape=(
                jax.ShapeDtypeStruct(pair_grad.shape, BF16),
                jax.ShapeDtypeStruct(left.shape, F32),
                jax.ShapeDtypeStruct(right.shape, F32),
                jax.ShapeDtypeStruct(proj.shape, F32),
            ),
            in_specs=[vmem] * 5,
            out_specs=[vmem] * 4,
            scratch_shapes=scratch,
            compiler_params=pltpu.CompilerParams(
                collective_id=0, has_side_effects=True, vmem_limit_bytes=60 << 20),
        )(left, right, proj, bias.reshape(1, -1), pair_grad)
        if not share:
            proj_grad = proj_grad.reshape(CH, CH, PAIR).transpose(1, 0, 2).reshape(proj.shape)
            proj_grad = lax.psum(proj_grad, ("row", "col"))
        return pair_out, left_grad, right_grad, proj_grad

    return jax.shard_map(
        step,
        mesh=mesh,
        in_specs=(P("col", "row"), P("row", "col"), P(), P(), P("row", "col", None)),
        out_specs=(P("row", "col", None), P("col", "row"), P("row", "col"), P()),
        check_vma=False,
    )
```

```python
import functools

import jax
import jax.numpy as jnp
from jax import lax
from jax.experimental import pallas as pl
from jax.experimental.pallas import tpu as pltpu
from jax.sharding import PartitionSpec as P

CH = 32
PAIR = 128
LANES = 128
PACK = LANES // CH
WIDE = PACK * LANES
TILE = 256
LONG = 512
PARTS = 2
MESH = pl.DeviceIdType.MESH
F32 = jnp.float32
BF16 = jnp.bfloat16


def inner_size(n):
    inner = 1
    while inner * inner * 4 <= n and n % (inner * 2) == 0:
        inner *= 2
    return inner


def dot(a, b):
    return jnp.dot(a, b, preferred_element_type=F32)


def aligned(index, size):
    return pl.ds(pl.multiple_of(index * size, size), size)


def kernel(
    R, C, share,
    left, right, proj, bias, pair_grad,
    pair_out, left_out, right_out, proj_out,
    lbuf, rbuf, lfull, ltrans, rtrans, rperm_t, rperm,
    pfull, spread, spread_t, outer, gpre, gpre_t, gouter,
    pterm, psend, precv, psum, pshare, pparts, pgather,
    rtmp, rown, rsend, rparts, lown, lsend, lxparts, lzsend, lzparts,
    s_lz, r_lz, s_lx, r_lx, s_rg, r_rg,
    s_pc, r_pc, s_ps, r_ps, s_pa, r_pa, s_pe, r_pe,
    s_rs, r_rs, s_lsx, r_lsx, s_lsz, r_lsz,
):
    C2 = inner_size(C)
    C1 = C // C2
    row, col = lax.axis_index("row"), lax.axis_index("col")
    z, x = col // C2, lax.rem(col, C2)
    seqs = lfull.shape[0]
    lwide = left.shape[1]
    rwide = right.shape[1]
    cols_here = rwide // CH
    groups = lwide // LANES
    rows = groups * cols_here
    scale = 1.0 / seqs

    def send(src, dst, ssem, rsem, to_row, to_col):
        return pltpu.make_async_remote_copy(
            src_ref=src, dst_ref=dst, send_sem=ssem, recv_sem=rsem,
            device_id=(to_row, to_col), device_id_type=MESH,
        )

    def zpeer(d):
        return lax.rem(z + d, C1)

    def xpeer(d):
        return lax.rem(x + d, C2)

    def rpeer(d):
        return lax.rem(row + d, R)

    barrier = pltpu.get_barrier_semaphore()
    for d in range(1, R):
        pl.semaphore_signal(barrier, inc=1, device_id=(rpeer(d), col), device_id_type=MESH)
    for d in range(1, C2):
        pl.semaphore_signal(
            barrier, inc=1, device_id=(row, z * C2 + xpeer(d)), device_id_type=MESH)
    for d in range(1, C1):
        pl.semaphore_signal(
            barrier, inc=1, device_id=(row, zpeer(d) * C2 + x), device_id_type=MESH)
    pl.semaphore_wait(barrier, R - 1 + C1 - 1 + C2 - 1)

    pending = []

    def go(copy):
        copy.start()
        pending.append(copy)
        return copy

    lchunk = lwide // PARTS
    for p in range(PARTS):
        piece = left.at[:, p * lchunk:(p + 1) * lchunk]
        for d in range(1, C1):
            go(send(
                piece, lbuf.at[p, col], s_lz.at[p, d - 1], r_lz.at[p, d - 1],
                row, zpeer(d) * C2 + x))
        for d in range(1, C2):
            go(send(
                piece, lbuf.at[p, col], s_lx.at[p, d - 1, 0], r_lx.at[p, d - 1, 0],
                row, z * C2 + xpeer(d)))
        if p == 0:
            for d in range(1, R):
                go(send(right, rbuf.at[row], s_rg.at[d - 1], r_rg.at[d - 1], rpeer(d), col))

    for p in range(PARTS):
        lbuf[p, col] = left[:, p * lchunk:(p + 1) * lchunk]
    rbuf[row] = right[...]
    pfull[...] = proj[...].astype(F32)
    lane_of = lax.broadcasted_iota(jnp.int32, (LANES, LANES), 1) // CH
    zero = jnp.zeros((CH, LANES), BF16)

    @pl.loop(0, CH)
    def _(e):
        block = pfull[pl.ds(e, CH, stride=CH), :]
        narrow = block.astype(BF16)
        spread[aligned(e, LANES), :] = jnp.concatenate(
            [
                jnp.concatenate([narrow if a == b else zero for b in range(PACK)], axis=1)
                for a in range(PACK)
            ],
            axis=0,
        )
        turned = jnp.concatenate([block] * PACK, axis=0).T
        for a in range(PACK):
            spread_t[a * LANES:(a + 1) * LANES, aligned(e, LANES)] = jnp.where(
                lane_of == a, turned, 0.0
            ).astype(BF16)

    def pass_on(p):
        for d in range(1, C1):
            block = lax.rem(z + C1 - d, C1) * C2 + x
            send(
                lbuf.at[p, block], lbuf.at[p, block], s_lz.at[p, d - 1], r_lz.at[p, d - 1],
                row, col).wait_recv()
            for k in range(1, C2):
                go(send(
                    lbuf.at[p, block], lbuf.at[p, block], s_lx.at[p, k - 1, d],
                    r_lx.at[p, k - 1, d], row, z * C2 + xpeer(k)))

    def arrive(p):
        for d in range(C1):
            for k in range(1, C2):
                block = lax.rem(z + C1 - d, C1) * C2 + lax.rem(x + C2 - k, C2)
                send(
                    lbuf.at[p, block], lbuf.at[p, block], s_lx.at[p, k - 1, d],
                    r_lx.at[p, k - 1, d], row, col).wait_recv()
        lfull[:, p * lchunk:(p + 1) * lchunk] = (
            lbuf[p].astype(F32).reshape(seqs, lchunk).astype(BF16))

    pass_on(0)
    for d in range(1, R):
        source = lax.rem(row + R - d, R)
        send(right, rbuf.at[source], s_rg.at[d - 1], r_rg.at[d - 1], row, col).wait_recv()

    rtrans[...] = rbuf[...].astype(F32).reshape(seqs, rwide).T

    @pl.loop(0, CH)
    def _(e):
        rperm_t[aligned(e, cols_here), :] = rtrans[
            pl.ds(e, cols_here, stride=CH), :].astype(BF16)

    rperm[...] = rperm_t[...].astype(F32).T.astype(BF16)

    wide_bias = jnp.concatenate([bias[...]] * PACK, axis=1)
    per = TILE // cols_here
    share_rows = rows // PARTS

    for p in range(PARTS):
        arrive(p)
        if p + 1 < PARTS:
            pass_on(p + 1)

        @pl.loop(p * lchunk // LONG, (p + 1) * lchunk // LONG)
        def _(t):
            part = (dot(rperm_t[...], lfull[:, aligned(t, LONG)]) * scale).astype(BF16)
            for h in range(LONG // LANES):
                for e in range(CH):
                    outer[
                        aligned(t * (LONG // LANES) + h, cols_here), e * LANES:(e + 1) * LANES
                    ] = part[e * cols_here:(e + 1) * cols_here, h * LANES:(h + 1) * LANES]

        @pl.loop(p * share_rows // TILE, (p + 1) * share_rows // TILE)
        def _(t):
            preact = dot(outer[aligned(t, TILE), :], spread[...]) + wide_bias
            active = jnp.maximum(preact, 0.0)
            square = (active * active).astype(BF16)
            for g in range(per):
                for a in range(PACK):
                    token = (t * per + g) * PACK + a
                    here = slice(g * cols_here, (g + 1) * cols_here)
                    there = slice(a * LANES, (a + 1) * LANES)
                    pair_out[token] = square[here, there]
                    gpre[aligned(t * per + g, cols_here), there] = (
                        pair_grad[token].astype(F32) * 2.0 * active[here, there]).astype(BF16)
            gpre_t[:, aligned(t, TILE)] = gpre[aligned(t, TILE), :].astype(F32).T.astype(BF16)

    @pl.loop(0, CH * LANES // LONG)
    def _(t):
        part = dot(gpre_t[...], outer[:, aligned(t, LONG)])
        for h in range(LONG // LANES):
            lanes = slice(h * LANES, (h + 1) * LANES)
            picked = part[:LANES, lanes]
            for a in range(1, PACK):
                picked = jnp.where(lane_of == a, part[a * LANES:(a + 1) * LANES, lanes], picked)
            turned = picked.T
            total = turned[:CH]
            for a in range(1, PACK):
                total = total + turned[a * CH:(a + 1) * CH]
            pterm[aligned(t * (LONG // LANES) + h, CH), :] = total

    if share:
        half = pterm.shape[0] // 2
        core = lax.rem(row, 2)
        other = row + 1 - 2 * core
        count = half // share
        me = (row // 2) * C + col
        mine = pterm[aligned(core, half), :]
        psend[...] = pterm[aligned(1 - core, half), :].astype(BF16)
        swap = go(send(psend, precv, s_pc, r_pc, other, col))

    if share:
        def owner(k):
            return (k // C) * 2 + core, lax.rem(k, C)

        def spread_sum():
            swap.wait_recv()
            both = (pterm[aligned(core, half), :] + precv[...].astype(F32)).reshape(count, share, PAIR)
            psum[...] = both
            pshare[...] = both.astype(BF16)
            scatter = []
            for d in range(1, count):
                k = lax.rem(me + d, count)
                scatter.append(go(send(
                    pshare.at[k], pparts.at[d - 1], s_ps.at[d - 1], r_ps.at[d - 1], *owner(k))))
            return scatter

    chunk_groups = groups // PARTS
    inner = {}
    for p in range(PARTS):

        @pl.loop(0, CH * LANES // LONG)
        def _(t):
            part = dot(
                gpre[p * share_rows:(p + 1) * share_rows, :], spread_t[:, aligned(t, LONG)]
            ).astype(BF16)
            for h in range(LONG // LANES):
                for g in range(chunk_groups):
                    lanes = slice((p * chunk_groups + g) * LANES, (p * chunk_groups + g + 1) * LANES)
                    gouter[aligned(t * (LONG // LANES) + h, cols_here), lanes] = (
                        part[g * cols_here:(g + 1) * cols_here, h * LANES:(h + 1) * LANES])

        @pl.loop(0, lchunk // LONG)
        def _(t):
            at = aligned(p * (lchunk // LONG) + t, LONG)
            part = (dot(rperm[...], gouter[:, at]) * scale).reshape(C, seqs // C, LONG)
            lown[p, :, :, aligned(t, LONG)] = part
            lsend[p, :, :, aligned(t, LONG)] = part.astype(BF16)

        for d in list(range(1, C1)) + [0]:
            for k in range(1, C2):
                inner[p, d, k] = go(send(
                    lsend.at[p, zpeer(d) * C2 + xpeer(k)], lxparts.at[p, k - 1, d],
                    s_lsx.at[p, k - 1, d], r_lsx.at[p, k - 1, d], row, z * C2 + xpeer(k)))

        if p == 0 and share:
            scatter = spread_sum()

    ltrans[...] = lfull[...].astype(F32).T.astype(BF16)

    @pl.loop(0, CH * cols_here // TILE)
    def _(t):
        part = dot(gouter[aligned(t, TILE), :], ltrans[...]) * scale
        for k in range(per):
            rtmp[pl.ds(t * per + k, cols_here, stride=CH), :] = (
                part[k * cols_here:(k + 1) * cols_here])

    turned = rtmp[...].T.reshape(R, seqs // R, rwide)
    rown[...] = turned
    rsend[...] = turned.astype(BF16)
    rights = [
        go(send(rsend.at[rpeer(d)], rparts.at[d - 1], s_rs.at[d - 1], r_rs.at[d - 1], rpeer(d), col))
        for d in range(1, R)
    ]

    outers = {}

    def pass_sums(p):
        for d in range(1, C1):
            total = lown[p, zpeer(d) * C2 + x]
            for k in range(1, C2):
                inner[p, d, k].wait_recv()
                total = total + lxparts[p, k - 1, d].astype(F32)
            lzsend[p, d - 1] = total.astype(BF16)
            outers[p, d] = go(send(
                lzsend.at[p, d - 1], lzparts.at[p, d - 1], s_lsz.at[p, d - 1],
                r_lsz.at[p, d - 1], row, zpeer(d) * C2 + x))

    pass_sums(0)

    if share:
        for copy in scatter:
            copy.wait_recv()
        total = psum[me]
        for d in range(1, count):
            total = total + pparts[d - 1].astype(F32)
        pgather[core, me] = total.astype(BF16)
        for d in range(1, count):
            k = lax.rem(me + d, count)
            go(send(
                pgather.at[core, me], pgather.at[core, me], s_pa.at[d - 1], r_pa.at[d - 1],
                *owner(k)))
    else:
        proj_out[...] = pterm[...]

    for p in range(1, PARTS):
        pass_sums(p)

    for copy in rights:
        copy.wait_recv()
    total = rown[row]
    for d in range(1, R):
        total = total + rparts[d - 1].astype(F32)
    right_out[...] = total

    if share:
        for d in range(1, count):
            k = lax.rem(me + count - d, count)
            send(
                pgather.at[core, me], pgather.at[core, k], s_pa.at[d - 1], r_pa.at[d - 1],
                *owner(k)).wait_recv()
        swap = go(send(pgather.at[core], pgather.at[core], s_pe, r_pe, other, col))

    for p in range(PARTS):
        total = lown[p, col]
        for k in range(1, C2):
            inner[p, 0, k].wait_recv()
            total = total + lxparts[p, k - 1, 0].astype(F32)
        for d in range(1, C1):
            outers[p, d].wait_recv()
            total = total + lzparts[p, d - 1].astype(F32)
        left_out[:, p * lchunk:(p + 1) * lchunk] = total

    if share:
        send(pgather.at[core], pgather.at[1 - core], s_pe, r_pe, other, col).wait_recv()
        rtmp_rows = pgather[...].astype(F32).reshape(2 * half, PAIR)
        pfull[...] = rtmp_rows

        @pl.loop(0, CH)
        def _(e):
            proj_out[pl.ds(e, CH, stride=CH), :] = pfull[aligned(e, CH), :]

    for copy in pending:
        copy.wait_send()


def solution(mesh):
    R, C = mesh.shape["row"], mesh.shape["col"]

    def step(left, right, proj, bias, pair_grad):
        lseq, lwide = left.shape
        rseq, rwide = right.shape
        seqs = lseq * C
        outer_size = proj.shape[0]
        cols_here = rwide // CH
        rows = lwide // LANES * cols_here
        C2 = inner_size(C)
        C1 = C // C2
        lchunk = lwide // PARTS
        share = outer_size // (R * C) if R % 2 == 0 else 0
        if share % 16:
            share = 0
        half = outer_size // 2
        keep = share or half
        count = half // keep
        some = max(count - 1, 1)
        dma = pltpu.SemaphoreType.DMA
        V = pltpu.VMEM
        scratch = [
            V((PARTS, C, lseq, lchunk), BF16), V((R, rseq, rwide), BF16), V((seqs, lwide), BF16),
            V((lwide, seqs), BF16), V((rwide, seqs), F32), V((rwide, seqs), BF16),
            V((seqs, rwide), BF16),
            V((outer_size, PAIR), F32), V((PACK * outer_size, WIDE), BF16),
            V((WIDE, PACK * outer_size), BF16), V((rows, PACK * outer_size), BF16),
            V((rows, WIDE), BF16), V((WIDE, rows), BF16), V((rwide, lwide), BF16),
            V((outer_size, PAIR), F32), V((half, PAIR), BF16), V((half, PAIR), BF16),
            V((count, keep, PAIR), F32), V((count, keep, PAIR), BF16),
            V((some, keep, PAIR), BF16), V((2, count, keep, PAIR), BF16),
            V((rwide, seqs), F32), V((R, rseq, rwide), F32), V((R, rseq, rwide), BF16),
            V((R - 1, rseq, rwide), BF16),
            V((PARTS, C, lseq, lchunk), F32), V((PARTS, C, lseq, lchunk), BF16),
            V((PARTS, C2 - 1, C1, lseq, lchunk), BF16), V((PARTS, C1 - 1, lseq, lchunk), BF16),
            V((PARTS, C1 - 1, lseq, lchunk), BF16),
            dma((PARTS, C1 - 1)), dma((PARTS, C1 - 1)),
            dma((PARTS, C2 - 1, C1)), dma((PARTS, C2 - 1, C1)),
            dma((R - 1,)), dma((R - 1,)),
            dma, dma, dma((some,)), dma((some,)), dma((some,)), dma((some,)), dma, dma,
            dma((R - 1,)), dma((R - 1,)),
            dma((PARTS, C2 - 1, C1)), dma((PARTS, C2 - 1, C1)),
            dma((PARTS, C1 - 1)), dma((PARTS, C1 - 1)),
        ]
        vmem = pl.BlockSpec(memory_space=pltpu.VMEM)
        pair_out, left_grad, right_grad, proj_grad = pl.pallas_call(
            functools.partial(kernel, R, C, share),
            out_shape=(
                jax.ShapeDtypeStruct(pair_grad.shape, BF16),
                jax.ShapeDtypeStruct(left.shape, F32),
                jax.ShapeDtypeStruct(right.shape, F32),
                jax.ShapeDtypeStruct(proj.shape, F32),
            ),
            in_specs=[vmem] * 5,
            out_specs=[vmem] * 4,
            scratch_shapes=scratch,
            compiler_params=pltpu.CompilerParams(
                collective_id=0, has_side_effects=True, vmem_limit_bytes=60 << 20),
        )(left, right, proj, bias.reshape(1, -1), pair_grad)
        if not share:
            proj_grad = proj_grad.reshape(CH, CH, PAIR).transpose(1, 0, 2).reshape(proj.shape)
            proj_grad = lax.psum(proj_grad, ("row", "col"))
        return pair_out, left_grad, right_grad, proj_grad

    return jax.shard_map(
        step,
        mesh=mesh,
        in_specs=(P("col", "row"), P("row", "col"), P(), P(), P("row", "col", None)),
        out_specs=(P("row", "col", None), P("col", "row"), P("row", "col"), P()),
        check_vma=False,
    )
```
